256 devices in a mesh: section: 4 (over z_lo, core), expert: 64 (over z_hi, y, x).
Axes of the slice: x: 4, y: 4, z: 8 (z_hi: 4, z_lo: 2; z = z_hi * 2 + z_lo), core: 2. Of those that a mesh axis runs over, the one named last changes fastest.
Arguments:
- grad_out: bfloat16 [4, 8192, 3584], P('section', 'expert'), may hold values from -6 to 6
- expert_ids: int32 [4, 8192, 8], P('section', 'expert'), may hold values from 0 to 63, all different within a row; in each aligned block of 128 rows (0 to 127, 128 to 255, ..., all dimensions but the last counted through in order) at most 20 rows name the same one
- gate_weights: bfloat16 [4, 8192, 8], P('section', 'expert'), may hold values from 0.019897461 to 0.5
- down_weight: bfloat16 [4, 64, 1024, 3584], P('section', 'expert'), may hold values from -0.09375 to 0.09375
- hidden_saved: bfloat16 [4, 64, 64, 20, 1024], P('section', 'expert'), may hold values from -0.19921875 to 0.19921875
Outputs:
- hidden_grad: bfloat16 [4, 64, 64, 20, 1024], P('section', 'expert')
- gate_grad: float32 [4, 8192, 8], P('section', 'expert')
The draws below stay inside these ranges and needn't reach their ends.
Inputs may be any that keep to these rules, and one draw needn't show every extreme that they name: `expert_ids`: each token names 8 distinct experts; among the tokens of one index of expert in one section, no expert is named by more than 20 of them, a bound that some block reaches.
All inputs are finite; a program needn't handle non-finite values.
Results may differ from the reference program's by a relative error of at most 0.001.
Values may be sent and summed in bfloat16 or wider, within the bound.
No kernel may reach another device: no remote copies, remote signals or barrier semaphores. Data moves between devices by JAX's collectives and lax.ppermute only.
A program may use at most 128 MiB of HBM per device.

```python
import math
import jax
import jax.numpy as jnp
import numpy as np
from jax import lax

D = 3584
HID = 1024
TOP = 8
TOK_DEV = 128
SECTIONS = 4
EXPERTS = 64
TOKENS = 8192
MOST = 20
N_EXPERT = 64


def level_of(rng, dims, pieces, smallest, largest):
    level = 1.0
    for axis_at, blocks in pieces:
        heights = jax.random.uniform(jax.random.fold_in(jax.random.fold_in(rng, 6), axis_at), (blocks,), jnp.float32, smallest / len(pieces), largest / len(pieces))
        level = level * jnp.repeat(jnp.exp(heights), dims[axis_at] // blocks).reshape((-1,) + (1,) * (len(dims) - 1 - axis_at))
    return level


def routed_block(key, own, number, rows, number_of, top, most, lean):
    ranking = jax.random.permutation(key, number_of)
    crowded, usual = shares(number_of, rows * top, most, lean, True), shares(number_of, rows * top, most, lean, False)
    places = jnp.arange(number_of)

    def named(sizes, offset_by):
        used = int((sizes > 0).sum())
        fixed = max(1, used // 4)
        moved = fixed + (places - fixed + offset_by * (used - fixed)) % max(1, number_of - fixed)
        return jnp.zeros((number_of,), jnp.int32).at[ranking[jnp.where(places < fixed, places, moved)]].set(jnp.asarray(sizes, jnp.int32))

    sizes = jnp.where(number % 4 == 0, named(crowded, number // 4), named(usual, number - number // 4 - 1))
    mixed = jax.random.permutation(jax.random.fold_in(own, 3), number_of)
    giver, receiver = mixed[0:number_of // 2 * 2:2], mixed[1:number_of // 2 * 2:2]
    slack = jnp.minimum(sizes[giver] - 1, most - sizes[receiver]) // 2
    slack = jnp.where((giver == ranking[0]) | (receiver == ranking[0]) | (sizes[receiver] == 0), 0, jnp.maximum(slack, 0))
    moved = jax.random.randint(jax.random.fold_in(own, 4), (number_of // 2,), 0, 1 << 20) % (slack + 1)
    sizes = sizes.at[giver].add(-moved).at[receiver].add(moved)
    items = jnp.searchsorted(jnp.cumsum(sizes), jnp.arange(rows * top), side="right").astype(jnp.int32)
    table = items.reshape(top, rows).T
    table = table[jax.random.permutation(jax.random.fold_in(own, 1), rows)]
    offset_by = jax.random.randint(jax.random.fold_in(own, 2), (rows, 1), 0, top)
    return jnp.take_along_axis(table, (jnp.arange(top)[None, :] + offset_by) % top, axis=1)


def shares(number_of, total, reach, lean, full):
    loads = [(1 << 20) // math.isqrt(grade ** lean) + 1 for grade in range(1, number_of + 1)]
    largest = reach if full else min(reach, max(-(-total // number_of), total * loads[0] // sum(loads)))
    least = 1 if total - largest >= number_of - 1 else 0
    counts, spare = [largest] + [least] * (number_of - 1), total - largest - least * (number_of - 1)
    while spare > 0:
        candidates = [i for i in range(1, number_of) if counts[i] < largest] or [i for i in range(1, number_of) if counts[i] < reach]
        mass, budget = sum([loads[i] for i in candidates]), spare
        for i in candidates:
            addition = min(reach - counts[i], max(1, budget * loads[i] // mass), spare)
            counts[i] = counts[i] + addition
            spare = spare - addition
    return np.array(counts)


def bell_draw(stream_key, dims, spread, limit, split=(), kind=jnp.bfloat16):
    entries = spread * jax.random.normal(stream_key, dims, jnp.float32)
    if split:
        entries = entries * level_of(stream_key, dims, split, -0.22, 0.18)
    return jnp.clip(entries, -limit, limit).astype(kind)


def setup_inputs(seed: int = 0) -> dict:
    splits = jax.random.split(jax.random.key(seed), 6)
    grad_out = bell_draw(splits[0], (SECTIONS, TOKENS, D), 1.0, 6.0, ((0, 4), (1, 64)))
    expert_ids_keys = jax.random.split(jax.random.fold_in(splits[1], 1), SECTIONS * TOKENS // TOK_DEV)
    expert_ids_turns = jax.random.permutation(jax.random.fold_in(splits[1], 3), SECTIONS * TOKENS // TOK_DEV)
    expert_ids = jax.vmap(lambda own, number: routed_block(jax.random.fold_in(splits[1], 2), own, number, TOK_DEV, EXPERTS, TOP, MOST, 2))(expert_ids_keys, expert_ids_turns).reshape((SECTIONS, TOKENS, TOP))
    gate_weights = jnp.clip(jnp.exp(math.log(0.5) - 3.224016 * jax.random.uniform(splits[2], (SECTIONS, TOKENS, TOP), jnp.float32) ** level_of(splits[2], (SECTIONS, TOKENS, TOP), ((0, 4), (1, 64)), -0.2, 0.2)), 0.019897461, 0.5).astype(jnp.bfloat16)
    down_weight = bell_draw(splits[3], (SECTIONS, EXPERTS, HID, D), D ** -0.5, 0.09375, ((0, 4), (1, 64)))
    hidden_saved = bell_draw(splits[4], (SECTIONS, EXPERTS, N_EXPERT, MOST, HID), 0.03125, 0.19921875, ((0, 4), (1, 64)))
    return dict(grad_out=grad_out, expert_ids=expert_ids, gate_weights=gate_weights, down_weight=down_weight, hidden_saved=hidden_saved)


def slot_ranks(ids_block):
    flat = ids_block.reshape(-1).astype(jnp.int32)
    onehot = (flat[:, None] == jnp.arange(EXPERTS, dtype=jnp.int32)[None, :]).astype(jnp.int32)
    rank = jnp.sum(jnp.cumsum(onehot, 0) * onehot, 1) - 1
    return flat, rank.astype(jnp.int32)


def reference(grad_out, expert_ids, gate_weights, down_weight, hidden_saved):
    incoming = jnp.roll(grad_out, -1, axis=0)
    slots = TOK_DEV * TOP
    total = EXPERTS * N_EXPERT * MOST
    grads_all = []
    gates_all = []
    for section_num in range(SECTIONS):
        flat, rank = jax.vmap(slot_ranks)(expert_ids[section_num].reshape(N_EXPERT, TOK_DEV, TOP))
        source = jnp.arange(N_EXPERT, dtype=jnp.int32)[:, None]
        token = source * TOK_DEV + (jnp.arange(slots, dtype=jnp.int32) // TOP)[None, :]
        dest = ((flat * N_EXPERT + source) * MOST + rank).reshape(-1)
        token_of = jnp.zeros((total,), jnp.int32).at[dest].set(token.reshape(-1))
        weight_of = jnp.zeros((total,), jnp.bfloat16).at[dest].set(gate_weights[section_num].reshape(-1))
        live_of = jnp.zeros((total,), jnp.bool_).at[dest].set(True)
        section_grad = incoming[section_num]
        section_down = down_weight[section_num]
        section_hidden = hidden_saved[section_num]

        def per_expert(expert_num):
            start = expert_num * (N_EXPERT * MOST)
            index = lax.dynamic_slice_in_dim(token_of, start, N_EXPERT * MOST)
            live = lax.dynamic_slice_in_dim(live_of, start, N_EXPERT * MOST)
            weight = lax.dynamic_slice_in_dim(weight_of, start, N_EXPERT * MOST)
            rows = jnp.where(live[:, None], section_grad[index], jnp.zeros((), jnp.bfloat16))
            back = lax.dot_general(rows, section_down[expert_num], (((1,), (1,)), ((), ())), preferred_element_type=jnp.float32)
            hidden_grad = (weight.astype(jnp.float32)[:, None] * back).astype(jnp.bfloat16)
            saved = section_hidden[expert_num].reshape(N_EXPERT * MOST, HID).astype(jnp.float32)
            slot_grad = jnp.sum(saved * back, axis=1)
            return hidden_grad.reshape(N_EXPERT, MOST, HID), slot_grad

        grads, slot_grads = lax.map(per_expert, jnp.arange(EXPERTS, dtype=jnp.int32))
        grads_all.append(grads)
        gates_all.append(slot_grads.reshape(-1)[dest].reshape(TOKENS, TOP))
    return jnp.stack(grads_all), jnp.stack(gates_all)
```

```python
import functools

import jax
import jax.numpy as jnp
from jax import lax
from jax.experimental import pallas as pl
from jax.experimental.pallas import tpu as pltpu
from jax.sharding import Mesh
from jax.sharding import PartitionSpec as P

RING = 4
MAIN = 16
F32 = jnp.float32
BF16 = jnp.bfloat16
HIGH = lax.Precision.HIGHEST


def iota(shape, dim):
    return lax.broadcasted_iota(jnp.int32, shape, dim)


def ranks_of(ids, experts):
    match = jnp.zeros(experts.shape, F32)
    for k in range(ids.shape[0]):
        match = jnp.where(ids[k : k + 1, :] == experts, 1.0, match)
    tokens = ids.shape[1]
    before = jnp.where(iota((tokens, tokens), 0) < iota((tokens, tokens), 1), 1.0, 0.0).astype(BF16)
    rank = jnp.dot(match.astype(BF16), before, preferred_element_type=F32)
    return jnp.where(match > 0.5, rank, -1.0)


def spread(rank, rows_per):
    n, total = rank.shape[0], rank.shape[0] * rows_per
    pick = jnp.where(iota((total, n), 0) // rows_per == iota((total, n), 1), 1.0, 0.0).astype(BF16)
    return jnp.dot(pick, rank.astype(BF16), preferred_element_type=F32)


def own_index_kernel(ring_ref, meta_ref, rank_ref, pick_ref):
    top = meta_ref.shape[0] // 2
    experts, tokens = rank_ref.shape
    plane = experts // RING
    ids = meta_ref[0:top, :].astype(F32)
    rank_ref[...] = ranks_of(ids, iota((experts, tokens), 0).astype(F32))
    first = ring_ref[0] * plane
    rank = ranks_of(ids, (iota((plane, tokens), 0) + first).astype(F32))
    rows = plane * MAIN
    slot = (iota((rows, tokens), 0) % MAIN).astype(F32)
    pick_ref[...] = jnp.where(spread(rank, MAIN) == slot, 1.0, 0.0).astype(BF16)


def index_kernel(most, ring_ref, m0_ref, m1_ref, m2_ref, m3_ref, side_ref, far_ref, rest_ref, weight_ref):
    top = m0_ref.shape[0] // 2
    tokens = m0_ref.shape[1]
    plane = far_ref.shape[0] // MAIN
    lanes = weight_ref.shape[1]
    experts = (iota((plane, tokens), 0) + ring_ref[0] * plane).astype(F32)
    ranks, weights = [], None
    for j, ref in enumerate((m0_ref, m1_ref, m2_ref, m3_ref)):
        meta = ref[...].astype(F32)
        ids, gates = meta[0:top, :], meta[top : 2 * top, :]
        rank = ranks_of(ids, experts)
        ranks.append(rank)
        gate = jnp.zeros((plane, tokens), F32)
        for k in range(top):
            gate = jnp.where(ids[k : k + 1, :] == experts, gates[k : k + 1, :], gate)
        slots = jnp.zeros((plane, lanes), F32)
        for r in range(most):
            column = jnp.sum(jnp.where(rank == float(r), gate, 0.0), axis=1, keepdims=True)
            slots = jnp.where(iota((plane, lanes), 1) == r, column, slots)
        place = iota((plane * 8, plane), 0) == iota((plane * 8, plane), 1) * 8 + j
        placed = jnp.dot(
            jnp.where(place, 1.0, 0.0).astype(BF16), slots.astype(BF16), preferred_element_type=F32
        )
        weights = placed if weights is None else weights + placed
    weight_ref[...] = weights.astype(BF16)

    rows = plane * MAIN
    slot = (iota((rows, tokens), 0) % MAIN).astype(F32)
    far_ref[...] = jnp.where(spread(ranks[2], MAIN) == slot, 1.0, 0.0).astype(BF16)

    row = iota((2 * rows, tokens), 0)
    slot = (row % MAIN).astype(F32)
    for side, j in enumerate((1, 3)):
        keep = (spread(ranks[j], 2 * MAIN) == slot) & ((row // MAIN) % 2 == side)
        side_ref[:, side * tokens : (side + 1) * tokens] = jnp.where(keep, 1.0, 0.0).astype(BF16)

    extra = most - MAIN
    row = iota((plane * RING * extra, tokens), 0)
    slot = (MAIN + row % extra).astype(F32)
    for j in range(RING):
        keep = (spread(ranks[j], RING * extra) == slot) & ((row // extra) % RING == j)
        rest_ref[:, j * tokens : (j + 1) * tokens] = jnp.where(keep, 1.0, 0.0).astype(BF16)


def expert_kernel(
    offset, most, ring_ref, low_ref, high_ref, down_ref, saved_ref, weight_ref, *refs
):
    rest = offset is None
    if rest:
        s0, s1, s2, s3, _, grad_ref, slot_ref, column_ref, total_ref = refs
    elif offset == 0:
        grad_ref, slot_ref, column_ref, total_ref = refs
    else:
        _, grad_ref, slot_ref, column_ref, total_ref = refs
    step = pl.program_id(0)
    rows = column_ref.shape[0]
    half = low_ref.shape[-1]
    plane = weight_ref.shape[0] // 8
    lanes = weight_ref.shape[1]
    extra = most - MAIN
    ring = ring_ref[0]

    def decode(i):
        source = i // MAIN
        if rest:
            return source, (i // extra) % RING, MAIN + i % extra
        return source, jnp.full(i.shape, offset, jnp.int32), i % MAIN

    @pl.when(step == 0)
    def _():
        source, j, slot = decode(iota((rows, plane * 8), 0))
        pick = jnp.where(iota((rows, plane * 8), 1) == source * 8 + j, 1.0, 0.0).astype(BF16)
        spread_weight = jnp.dot(pick, weight_ref[...], preferred_element_type=F32)
        _, _, slot = decode(iota((rows, lanes), 0))
        column_ref[...] = jnp.sum(
            jnp.where(iota((rows, lanes), 1) == slot, spread_weight, 0.0), axis=1, keepdims=True
        )
        total_ref[...] = jnp.zeros_like(total_ref)

    dims = (((1,), (1,)), ((), ()))
    low = low_ref[...].reshape(rows, half)
    high = high_ref[...].reshape(rows, half)
    back = lax.dot_general(low, down_ref[:, :half], dims, preferred_element_type=F32)
    back += lax.dot_general(high, down_ref[:, half:], dims, preferred_element_type=F32)

    source, j, slot = decode(iota((rows, rows), 1))
    if rest:
        out_row = (slot - MAIN) * (plane * RING) + ((ring + j) % RING) * plane + source
    else:
        out_row = slot * plane + source
    move = jnp.where(iota((rows, rows), 0) == out_row, 1.0, 0.0).astype(BF16)

    grad = (column_ref[...] * back).astype(BF16)
    moved = jnp.dot(move, grad, preferred_element_type=F32).astype(BF16)
    grad_ref[...] = moved.reshape(grad_ref.shape)
    saved = saved_ref[...].reshape(rows, saved_ref.shape[-1])
    saved = lax.dot_general(move, saved, (((0,), (0,)), ((), ())), preferred_element_type=F32)
    total_ref[...] += jnp.sum(saved * back, axis=1, keepdims=True)

    @pl.when(step == pl.num_programs(0) - 1)
    def _():
        _, _, slot = decode(iota((rows, lanes), 0))
        wide = jnp.where(iota((rows, lanes), 1) == slot, total_ref[...], 0.0)
        count = RING * plane if rest else plane
        source, j, _ = decode(iota((count, rows), 1))
        row = iota((count, rows), 0)
        here = (row == j * plane + source) if rest else (row == source)
        slots = jnp.dot(
            jnp.where(here, 1.0, 0.0), wide, precision=HIGH, preferred_element_type=F32
        )
        if rest:
            for k, ref in enumerate((s0, s1, s2, s3)):
                slot_ref[(ring + k) % RING] = ref[...] + slots[k * plane : (k + 1) * plane, :]
        else:
            slot_ref[...] = slots


def gate_kernel(most, got_ref, rank_ref, meta_ref, out_ref):
    top = out_ref.shape[0]
    got, rank = got_ref[...], rank_ref[...]
    value = jnp.zeros(rank.shape, F32)
    for r in range(most):
        value = jnp.where(rank == float(r), got[:, r : r + 1], value)
    ids = meta_ref[0:top, :].astype(F32)
    experts = iota(rank.shape, 0).astype(F32)
    for k in range(top):
        out_ref[k : k + 1, :] = jnp.sum(
            jnp.where(ids[k : k + 1, :] == experts, value, 0.0), axis=0, keepdims=True
        )


def project(interpret, offset, most, ring, parts, down, saved, weight, before, prior):
    rest = offset is None
    hidden, width = down.shape
    half = width // 2
    slots, blocks, _ = saved.shape
    plane = blocks // RING
    rows = plane * MAIN
    tile = min(256, hidden)
    low, high, low_spec, high_spec = parts
    if rest:
        extra = most - MAIN
        grad_block = pl.BlockSpec((extra, blocks, tile), lambda n, ring: (MAIN // extra, 0, n))
    else:
        grad_block = pl.BlockSpec(
            (MAIN, plane, tile), lambda n, ring: (0, (ring[0] + offset) % RING, n)
        )
    slot_shape = (RING, plane, 128) if rest else (plane, 128)
    whole = lambda shape: pl.BlockSpec(shape, lambda n, ring: (0,) * len(shape))
    operands = [low, high, down, saved, weight]
    in_specs = [
        low_spec,
        high_spec,
        pl.BlockSpec((tile, width), lambda n, ring: (n, 0)),
        grad_block,
        whole(weight.shape),
    ]
    aliases = {}
    for slot in prior:
        operands.append(slot)
        in_specs.append(whole(slot.shape))
    if before is not None:
        aliases = {1 + len(operands): 0}
        operands.append(before)
        in_specs.append(pl.BlockSpec(memory_space=pl.ANY))
    return pl.pallas_call(
        functools.partial(expert_kernel, offset, most),
        grid_spec=pltpu.PrefetchScalarGridSpec(
            num_scalar_prefetch=1,
            grid=(hidden // tile,),
            in_specs=in_specs,
            out_specs=[grad_block, whole(slot_shape)],
            scratch_shapes=[pltpu.VMEM((rows, 1), F32), pltpu.VMEM((rows, 1), F32)],
        ),
        out_shape=[
            jax.ShapeDtypeStruct((slots, blocks, hidden), BF16),
            jax.ShapeDtypeStruct(slot_shape, F32),
        ],
        input_output_aliases=aliases,
        cost_estimate=pl.CostEstimate(
            flops=2 * rows * hidden * width,
            bytes_accessed=2 * hidden * width + 2 * rows * (width + 2 * hidden),
            transcendentals=0,
        ),
        compiler_params=pltpu.CompilerParams(vmem_limit_bytes=32 * 1024 * 1024),
        interpret=interpret,
        name="rest_rows" if rest else f"rows_{offset}",
    )(ring, *operands)


def small_call(kernel, ring, operands, outs, name, interpret):
    specs = [pl.BlockSpec(memory_space=pltpu.VMEM)] * len(operands)
    if ring is not None:
        operands = [ring] + operands
        specs = [pl.BlockSpec(memory_space=pltpu.SMEM)] + specs
    return pl.pallas_call(
        kernel,
        in_specs=specs,
        out_specs=[pl.BlockSpec(memory_space=pltpu.VMEM)] * len(outs),
        out_shape=outs,
        cost_estimate=pl.CostEstimate(flops=10**6, bytes_accessed=10**6, transcendentals=0),
        interpret=interpret,
        name=name,
    )(*operands)


def pick_rows(pick, rows):
    return jnp.dot(pick, rows, preferred_element_type=F32).astype(BF16)


def exchange(rows):
    plane = lax.axis_size("plane")
    split = rows.reshape(plane, -1, rows.shape[1])
    return lax.all_to_all(split, "plane", split_axis=0, concat_axis=0, tiled=True)


def local(interpret, grad_out, expert_ids, gate_weights, down_weight, hidden_saved):
    plane = lax.axis_size("plane")
    sections = lax.axis_size("section")
    blocks, most, hidden = hidden_saved.shape[2:]
    width = grad_out.shape[2]
    half = width // 2
    tokens, top = expert_ids.shape[1:]
    ring = lax.axis_index("ring").astype(jnp.int32).reshape(1)
    move = lambda j, x: lax.ppermute(x, "ring", [((i + j) % RING, i) for i in range(RING)])

    x0 = lax.ppermute(grad_out[0], "section", [(i, (i - 1) % sections) for i in range(sections)])
    meta0 = jnp.concatenate([expert_ids[0].T.astype(BF16), gate_weights[0].T], axis=0)
    metas = [meta0] + [move(j, meta0) for j in (1, 2, 3)]

    rows = plane * MAIN
    S = jax.ShapeDtypeStruct
    rank, pick0 = small_call(
        own_index_kernel, ring, [meta0], [S((blocks, tokens), F32), S((rows, tokens), BF16)],
        "own_index", interpret,
    )
    x0l, x0h = x0[:, :half], x0[:, half:]
    x1l, x3l = move(1, x0l), move(3, x0l)
    x1h, x3h = move(1, x0h), move(3, x0h)
    x2l, x2h = move(1, x1l), move(3, x3h)

    got0 = exchange(pick_rows(pick0, x0))
    pick_side, pick_far, pick_rest, weight = small_call(
        functools.partial(index_kernel, most), ring, metas,
        [
            S((2 * rows, 2 * tokens), BF16),
            S((rows, tokens), BF16),
            S((plane * RING * (most - MAIN), RING * tokens), BF16),
            S((plane * 8, 128), BF16),
        ],
        "index", interpret,
    )
    weight = exchange(weight).reshape(plane * 8, 128)
    got_l = exchange(pick_rows(pick_side, jnp.concatenate([x1l, x3l], axis=0)))
    got_h = exchange(pick_rows(pick_side, jnp.concatenate([x1h, x3h], axis=0)))
    x2 = jnp.concatenate([x2l, x2h], axis=1)
    got2 = exchange(pick_rows(pick_far, x2))
    x_all = jnp.concatenate(
        [x0, jnp.concatenate([x1l, x1h], 1), x2, jnp.concatenate([x3l, x3h], 1)], axis=0
    )
    got_rest = exchange(pick_rows(pick_rest, x_all))

    down = down_weight[0, 0]
    saved = hidden_saved[0, 0].transpose(1, 0, 2)
    part_specs = [pl.BlockSpec((rows, half), lambda n, ring, c=c: (0, c)) for c in range(2)]

    def both(got):
        flat = got.reshape(rows, width)
        return (flat, flat, *part_specs)

    def side(s):
        spec = pl.BlockSpec((plane, None, MAIN, half), lambda n, ring: (0, s, 0, 0))
        shape = (plane, 2, MAIN, half)
        return (got_l.reshape(shape), got_h.reshape(shape), spec, spec)

    run = functools.partial(project, interpret)
    grad, s0 = run(0, most, ring, both(got0), down, saved, weight, None, [])
    grad, s1 = run(1, most, ring, side(0), down, saved, weight, grad, [])
    grad, s3 = run(3, most, ring, side(1), down, saved, weight, grad, [])
    grad, s2 = run(2, most, ring, both(got2), down, saved, weight, grad, [])
    grad, slots = run(None, most, ring, both(got_rest), down, saved, weight, grad, [s0, s1, s2, s3])

    returned = lax.all_to_all(
        slots.reshape(blocks, 1, 128), ("ring", "plane"), split_axis=0, concat_axis=0, tiled=True
    )
    gate = small_call(
        functools.partial(gate_kernel, most), None, [returned.reshape(blocks, 128), rank, meta0],
        [S((top, tokens), F32)], "gate", interpret,
    )[0]
    return (grad.transpose(1, 0, 2)[None, None], gate.T[None])


def solution(mesh, interpret=False):
    sections, experts = mesh.devices.shape
    fine = Mesh(mesh.devices.reshape(sections, RING, experts // RING), ("section", "ring", "plane"))
    both = ("ring", "plane")
    in_specs = (
        P("section", both, None),
        P("section", both, None),
        P("section", both, None),
        P("section", both, None, None),
        P("section", both, None, None, None),
    )
    out_specs = (P("section", both, None, None, None), P("section", both, None))
    return jax.shard_map(
        functools.partial(local, interpret), mesh=fine, in_specs=in_specs, out_specs=out_specs, check_vma=False
    )
```
